32 devices in a mesh: gx: 16 (over z, y, core), gy: 2 (over x).
Axes of the slice: x: 2, y: 2, z: 4, core: 2. Of those that a mesh axis runs over, the one named last changes fastest.
Arguments:
- inputs: bfloat16 [128, 8192], P('gy', 'gx'), may hold values from -6 to 6
- gate_pre: bfloat16 [128, 28672], P('gx', 'gy'), may hold values from -8 to 8
- up_pre: bfloat16 [128, 28672], P('gx', 'gy'), may hold values from -6 to 6
- out_grad: bfloat16 [128, 8192], P('gy', 'gx'), may hold values from -6 to 6
- w_gate: bfloat16 [8192, 28672], P('gx', 'gy'), may hold values from -0.0625 to 0.0625
- w_up: bfloat16 [8192, 28672], P('gx', 'gy'), may hold values from -0.0625 to 0.0625
- w_down: bfloat16 [28672, 8192], P('gy', 'gx'), may hold values from -0.03125 to 0.03125
Outputs:
- grad_input: bfloat16 [128, 8192], P('gy', 'gx')
- grad_w_gate: bfloat16 [8192, 28672], P('gx', 'gy')
- grad_w_up: bfloat16 [8192, 28672], P('gx', 'gy')
- grad_w_down: bfloat16 [28672, 8192], P('gy', 'gx')
The draws below stay inside these ranges and needn't reach their ends.
All inputs are finite; a program needn't handle non-finite values.
Results may differ from the reference program's by a relative error of at most 0.017.
Values may be sent and summed in bfloat16 or wider, within the bound.
A program may use at most 256 MiB of HBM per device.

```python
import jax
import jax.numpy as jnp
from jax import lax

D = 8192
FF = 28672
TOKENS = 128
N_GX = 16


def with_spikes(array, key, source, target, parts, factor):
    owner, partner = [(jnp.arange(array.shape[axis_at]) // (array.shape[axis_at] // parts)).reshape([-1 if axis == axis_at else 1 for axis in range(array.ndim)]) for axis_at in (source, target)]
    chosen = jax.random.permutation(key, parts)[partner]
    strong = (owner == chosen) | (owner == (partner + parts // 2) % parts)
    return jnp.where(strong, factor * array, array)


def levels(own_key, extent, shards, least, top_value):
    level = 1.0
    for position, shards_of in shards:
        steps = jax.random.uniform(jax.random.fold_in(jax.random.fold_in(own_key, 6), position), (shards_of,), jnp.float32, least / len(shards), top_value / len(shards))
        level = level * jnp.repeat(jnp.exp(steps), extent[position] // shards_of).reshape((-1,) + (1,) * (len(extent) - 1 - position))
    return level


def bell_draw(stream_key, extent, width, most, cuts=(), held_as=jnp.bfloat16):
    drawn = width * jax.random.normal(stream_key, extent, jnp.float32)
    if cuts:
        drawn = drawn * levels(stream_key, extent, cuts, -0.22, 0.18)
    return jnp.clip(drawn, -most, most).astype(held_as)


def gaussian_with(rng, dims, spread, bound, split, heavy, held_as=jnp.bfloat16):
    values = spread * jax.random.normal(rng, dims, jnp.float32)
    if split:
        values = values * levels(rng, dims, split, -0.22, 0.18)
    return jnp.clip(with_spikes(values, jax.random.fold_in(rng, 3), *heavy), -bound, bound).astype(held_as)


def setup_inputs(seed: int = 0) -> dict:
    arg_keys = jax.random.split(jax.random.key(seed), 8)
    return {
        "inputs": bell_draw(arg_keys[0], (TOKENS, D), 1.0, 6.0, ((0, 2), (1, 16))),
        "gate_pre": bell_draw(arg_keys[1], (TOKENS, FF), 1.5, 8.0, ((0, 16), (1, 2))),
        "up_pre": bell_draw(arg_keys[2], (TOKENS, FF), 1.0, 6.0, ((0, 16), (1, 2))),
        "out_grad": gaussian_with(arg_keys[3], (TOKENS, D), 1.0, 6.0, ((0, 2), (1, 16)), (1, 0, 16, 2.0)),
        "w_gate": bell_draw(arg_keys[4], (D, FF), D ** -0.5, 0.0625, ((0, 16), (1, 2))),
        "w_up": bell_draw(arg_keys[5], (D, FF), D ** -0.5, 0.0625, ((0, 16), (1, 2))),
        "w_down": bell_draw(arg_keys[6], (FF, D), FF ** -0.5, 0.03125, ((0, 2), (1, 16))),
    }


def swiglu_back(d_hidden, gate_pre, up_pre):
    gate_val = gate_pre.astype(jnp.float32)
    up_val = up_pre.astype(jnp.float32)
    sig = jax.nn.sigmoid(gate_val)
    silu_val = gate_val * sig
    hidden = (silu_val * up_val).astype(jnp.bfloat16)
    d_up = (d_hidden * silu_val).astype(jnp.bfloat16)
    d_gate = (d_hidden * up_val * sig * (1.0 + gate_val * (1.0 - sig))).astype(jnp.bfloat16)
    return (d_gate, d_up, hidden)

def hidden_grad(out_grad, w_down):
    block_width = D // N_GX
    grad_blocks = out_grad.reshape(TOKENS, N_GX, block_width).transpose(1, 0, 2)
    down_blocks = w_down.reshape(FF, N_GX, block_width).transpose(1, 0, 2)

    def add_block(total, pieces):
        grad_block, down_block = pieces
        term = jnp.dot(grad_block, down_block.T, preferred_element_type=jnp.float32)
        rounded = lax.optimization_barrier(term.astype(jnp.bfloat16))
        return (total + rounded.astype(jnp.float32), None)
    start = jnp.zeros((TOKENS, FF), jnp.float32)
    total, _ = lax.scan(add_block, start, (grad_blocks, down_blocks))
    return total

def reference(inputs, gate_pre, up_pre, out_grad, w_gate, w_up, w_down):
    d_hidden = hidden_grad(out_grad, w_down)
    d_gate, d_up, hidden = swiglu_back(d_hidden, gate_pre, up_pre)
    grad_w_down = jnp.dot(hidden.T, out_grad, preferred_element_type=jnp.float32).astype(jnp.bfloat16)
    grad_w_gate = jnp.dot(inputs.T, d_gate, preferred_element_type=jnp.float32).astype(jnp.bfloat16)
    grad_w_up = jnp.dot(inputs.T, d_up, preferred_element_type=jnp.float32).astype(jnp.bfloat16)
    summed = jnp.dot(d_gate, w_gate.T, preferred_element_type=jnp.float32) + jnp.dot(d_up, w_up.T, preferred_element_type=jnp.float32)
    grad_input = summed.astype(jnp.bfloat16)
    return (grad_input, grad_w_gate, grad_w_up, grad_w_down)
```

```python
import functools

import jax
import jax.numpy as jnp
from jax import lax
from jax.experimental import pallas as pl
from jax.experimental.pallas import tpu as pltpu
from jax.sharding import PartitionSpec as P

MESH = pl.DeviceIdType.MESH
F32 = jnp.float32
BF16 = jnp.bfloat16
CHUNKS = 7
OUTER = 4


def exchange_kernel(
    sizes,
    x_ref, og_ref, gate_ref, up_ref, wd_ref,
    dh_ref, gates_ref, ups_ref, xs_ref, ogs_ref,
    w_buf, og_buf, part, core_in, sum_core, inner_in, sum_inner, outer_in, own,
    w_sem, local_sem, gy_send, gy_recv,
    rc_send, rc_recv, ri_send, ri_recv, ro_send, ro_recv,
    go_send, go_recv, gi_send, gi_recv, gc_send, gc_recv,
    ho_send, ho_recv, hi_send, hi_recv, hc_send, hc_recv,
    own_sem,
):
    A, B, G, K = sizes
    me = lax.axis_index("gx")
    gy = lax.axis_index("gy")
    core = lax.rem(me, 2)
    b = lax.rem(me // 2, B)
    a = me // (2 * B)
    cw = w_buf.shape[1]
    t = og_ref.shape[0]

    def index(ai, bi, ci):
        return (ai * B + bi) * 2 + ci

    def outer_peer(d):
        return lax.rem(a + d, A)

    def outer_source(d):
        return lax.rem(a + A - d, A)

    def inner_peer(d):
        return lax.rem(b + d, B)

    def inner_source(d):
        return lax.rem(b + B - d, B)

    def remote(src, dst, send, recv, gx_to, gy_to=None):
        return pltpu.make_async_remote_copy(
            src_ref=src, dst_ref=dst, send_sem=send, recv_sem=recv,
            device_id=(gx_to, gy if gy_to is None else gy_to), device_id_type=MESH,
        )

    sibling = index(a, b, 1 - core)

    barrier = pltpu.get_barrier_semaphore()
    pl.semaphore_signal(barrier, inc=1, device_id=(sibling, gy), device_id_type=MESH)
    for d in range(1, A):
        pl.semaphore_signal(barrier, inc=1, device_id=(index(outer_peer(d), b, core), gy), device_id_type=MESH)
    for d in range(1, B):
        pl.semaphore_signal(barrier, inc=1, device_id=(index(a, inner_peer(d), core), gy), device_id_type=MESH)
    for d in range(1, G):
        pl.semaphore_signal(barrier, inc=1, device_id=(me, lax.rem(gy + d, G)), device_id_type=MESH)
    pl.semaphore_wait(barrier, 1 + (A - 1) + (B - 1) + (G - 1))

    def w_copy(k, slot):
        return pltpu.make_async_copy(wd_ref.at[pl.ds(pl.multiple_of(k * cw, cw), cw)], w_buf.at[slot], w_sem.at[slot])

    w_copy(0, 0).start()
    w_copy(1, 1).start()

    def gy_copies(d):
        to = lax.rem(gy + d, G)
        return (
            remote(og_ref, og_buf.at[gy], gy_send.at[0, d - 1], gy_recv.at[0, d - 1], me, to),
            remote(x_ref, xs_ref.at[gy], gy_send.at[1, d - 1], gy_recv.at[1, d - 1], me, to),
        )

    locals_ = [
        pltpu.make_async_copy(og_ref, og_buf.at[gy], local_sem.at[0]),
        pltpu.make_async_copy(x_ref, xs_ref.at[gy], local_sem.at[1]),
        pltpu.make_async_copy(gate_ref, gates_ref.at[me], local_sem.at[2]),
        pltpu.make_async_copy(up_ref, ups_ref.at[me], local_sem.at[3]),
    ]
    locals_[0].start()
    for d in range(1, G):
        gy_copies(d)[0].start()

    def gather_ops(full, outer_s, outer_r, inner_s, inner_r, core_s, core_r):
        def to_outer(src, d):
            return remote(src, full(me), outer_s(d - 1), outer_r(d - 1), index(outer_peer(d), b, core))

        def to_inner(src, ai, d):
            s = index(ai, b, core)
            return remote(src, full(s), inner_s(d - 1, ai), inner_r(d - 1, ai), index(a, inner_peer(d), core))

        def to_core(src, ai, bi):
            s = index(ai, bi, core)
            return remote(src, full(s), core_s(ai * B + bi), core_r(ai * B + bi), sibling)

        return to_outer, to_inner, to_core

    def send_own(ops, src):
        to_outer, to_inner, to_core = ops
        for d in range(1, A):
            to_outer(src, d).start()
        for d in range(1, B):
            to_inner(src, a, d).start()
        to_core(src, a, b).start()

    def pass_outer(ops, full):
        to_outer, to_inner, to_core = ops
        for d in range(1, A):
            to_outer(full(me), d).wait_recv()
            ai = outer_source(d)
            src = full(index(ai, b, core))
            for e in range(1, B):
                to_inner(src, ai, e).start()
            to_core(src, ai, b).start()

    def pass_inner(ops, full):
        to_outer, to_inner, to_core = ops
        for e in range(1, B):
            bi = inner_source(e)
            for d in range(A):
                ai = outer_source(d)
                to_inner(full(me), ai, e).wait_recv()
                to_core(full(index(ai, bi, core)), ai, bi).start()

    def finish(ops, full):
        to_outer, to_inner, to_core = ops
        for d in range(1, A):
            to_outer(full(me), d).wait_send()
        for e in range(1, B):
            for ai in range(A):
                to_inner(full(me), ai, e).wait_send()
        for ai in range(A):
            for bi in range(B):
                to_core(full(me), ai, bi).wait()

    saved = []
    for g, out in enumerate((gates_ref, ups_ref)):
        full = functools.partial(lambda out, s: out.at[s], out)
        ops = gather_ops(
            full,
            functools.partial(lambda g, i: go_send.at[g, i], g),
            functools.partial(lambda g, i: go_recv.at[g, i], g),
            functools.partial(lambda g, i, j: gi_send.at[g, i, j], g),
            functools.partial(lambda g, i, j: gi_recv.at[g, i, j], g),
            functools.partial(lambda g, i: gc_send.at[g, i], g),
            functools.partial(lambda g, i: gc_recv.at[g, i], g),
        )
        saved.append((ops, full))

    send_own(saved[0][0], gate_ref)
    send_own(saved[1][0], up_ref)
    for d in range(1, G):
        gy_copies(d)[1].start()
    for copy in locals_[1:]:
        copy.start()
    locals_[0].wait()
    for d in range(1, G):
        gy_copies(d)[0].wait_recv()
    og_out = pltpu.make_async_copy(og_buf, ogs_ref, local_sem.at[4])
    og_out.start()

    def core_copy(k):
        return remote(part.at[k, :, :, 1 - core], core_in.at[k], rc_send.at[k], rc_recv.at[k], sibling)

    def inner_copy(k, e):
        return remote(
            sum_core.at[k, inner_peer(e)], inner_in.at[k, e - 1],
            ri_send.at[k, e - 1], ri_recv.at[k, e - 1], index(a, inner_peer(e), core),
        )

    def outer_copy(k, d):
        return remote(
            sum_inner.at[k, outer_peer(d)], outer_in.at[k, d - 1],
            ro_send.at[k, d - 1], ro_recv.at[k, d - 1], index(outer_peer(d), b, core),
        )

    def multiply(k, _):
        slot = lax.rem(k, 2)
        w_copy(k, slot).wait()
        og = og_buf[...].reshape(G * t, og_buf.shape[2])
        prod = lax.dot_general(og, w_buf[slot], (((1,), (1,)), ((), ())), preferred_element_type=F32)
        part[k] = prod.reshape(part.shape[1:]).astype(BF16)
        core_copy(k).start()

        @pl.when(k + 2 < K)
        def _():
            w_copy(k + 2, slot).start()
        return 0

    lax.fori_loop(0, K, multiply, 0)

    def add_core(k, _):
        core_copy(k).wait_recv()
        for bi in range(B):
            sum_core[k, bi] = (part[k, :, bi, core].astype(F32) + core_in[k, :, bi].astype(F32)).astype(BF16)
        for e in range(1, B):
            inner_copy(k, e).start()
        return 0

    lax.fori_loop(0, K, add_core, 0)
    for ops, full in saved:
        pass_outer(ops, full)

    def add_inner(k, _):
        total = sum_core[k, b].astype(F32)
        for e in range(1, B):
            inner_copy(k, e).wait_recv()
            total += inner_in[k, e - 1].astype(F32)
        sum_inner[k] = total.astype(BF16)
        for d in range(1, A):
            outer_copy(k, d).start()
        return 0

    lax.fori_loop(0, K, add_inner, 0)
    for ops, full in saved:
        pass_inner(ops, full)

    def hidden_ops(k):
        full = lambda s: dh_ref.at[k, s]
        return gather_ops(
            full,
            lambda i: ho_send.at[k, i], lambda i: ho_recv.at[k, i],
            lambda i, j: hi_send.at[k, i, j], lambda i, j: hi_recv.at[k, i, j],
            lambda i: hc_send.at[k, i], lambda i: hc_recv.at[k, i],
        ), full

    def own_copy(k):
        return pltpu.make_async_copy(own.at[k], dh_ref.at[k, me], own_sem.at[k])

    def add_outer(k, _):
        total = sum_inner[k, a].astype(F32)
        for d in range(1, A):
            outer_copy(k, d).wait_recv()
            total += outer_in[k, d - 1].astype(F32)
        own[k] = total.astype(BF16)
        send_own(hidden_ops(k)[0], own.at[k])
        own_copy(k).start()
        return 0

    lax.fori_loop(0, K, add_outer, 0)

    def forward_outer(k, _):
        pass_outer(*hidden_ops(k))
        return 0

    lax.fori_loop(0, K, forward_outer, 0)

    def forward_inner(k, _):
        pass_inner(*hidden_ops(k))
        return 0

    lax.fori_loop(0, K, forward_inner, 0)

    def close(k, _):
        finish(*hidden_ops(k))
        own_copy(k).wait()
        core_copy(k).wait_send()
        for e in range(1, B):
            inner_copy(k, e).wait_send()
        for d in range(1, A):
            outer_copy(k, d).wait_send()
        return 0

    lax.fori_loop(0, K, close, 0)
    for ops, full in saved:
        finish(ops, full)
    for copy in locals_[1:]:
        copy.wait()
    og_out.wait()
    for d in range(1, G):
        og_copy, x_copy = gy_copies(d)
        og_copy.wait_send()
        x_copy.wait()


def exchange(n, G, x, og, gate, up, wd):
    A = OUTER if n % (2 * OUTER) == 0 else 1
    B = n // (2 * A)
    K = CHUNKS
    t, dl = og.shape
    rows, ffl = gate.shape
    cw = ffl // K
    any_spec = pl.BlockSpec(memory_space=pl.ANY)
    dma = pltpu.SemaphoreType.DMA
    return pl.pallas_call(
        functools.partial(exchange_kernel, (A, B, G, K)),
        out_shape=(
            jax.ShapeDtypeStruct((K, n, rows, cw), BF16),
            jax.ShapeDtypeStruct((n, rows, ffl), BF16),
            jax.ShapeDtypeStruct((n, rows, ffl), BF16),
            jax.ShapeDtypeStruct((G, t, dl), BF16),
            jax.ShapeDtypeStruct((G, t, dl), BF16),
        ),
        in_specs=[any_spec] * 5,
        out_specs=(any_spec,) * 5,
        scratch_shapes=[
            pltpu.VMEM((2, cw, dl), BF16),
            pltpu.VMEM((G, t, dl), BF16),
            pltpu.VMEM((K, A, B, 2, rows, cw), BF16),
            pltpu.VMEM((K, A, B, rows, cw), BF16),
            pltpu.VMEM((K, B, A, rows, cw), BF16),
            pltpu.VMEM((K, max(B - 1, 1), A, rows, cw), BF16),
            pltpu.VMEM((K, A, rows, cw), BF16),
            pltpu.VMEM((K, max(A - 1, 1), rows, cw), BF16),
            pltpu.VMEM((K, rows, cw), BF16),
            dma((2,)), dma((5,)), dma((2, max(G - 1, 1))), dma((2, max(G - 1, 1))),
            dma((K,)), dma((K,)), dma((K, max(B - 1, 1))), dma((K, max(B - 1, 1))),
            dma((K, max(A - 1, 1))), dma((K, max(A - 1, 1))),
            dma((2, max(A - 1, 1))), dma((2, max(A - 1, 1))),
            dma((2, max(B - 1, 1), A)), dma((2, max(B - 1, 1), A)),
            dma((2, A * B)), dma((2, A * B)),
            dma((K, max(A - 1, 1))), dma((K, max(A - 1, 1))),
            dma((K, max(B - 1, 1), A)), dma((K, max(B - 1, 1), A)),
            dma((K, A * B)), dma((K, A * B)),
            dma((K,)),
        ],
        compiler_params=pltpu.CompilerParams(
            collective_id=0, has_side_effects=True, vmem_limit_bytes=32 * 2**20
        ),
    )(x, og, gate, up, wd)


def gate_up_kernel(x_ref, dh_ref, gate_ref, up_ref, wg_ref, wu_ref, gin_ref, gwg_ref, gwu_ref, xt, acc):
    step = pl.program_id(0)
    tokens, dl = x_ref.shape

    @pl.when(step == 0)
    def _():
        xt[...] = x_ref[...].astype(F32).T.astype(BF16)
        acc[...] = jnp.zeros_like(acc)

    width = gate_ref.shape[2]
    g = gate_ref[...].astype(F32).reshape(tokens, width)
    u = up_ref[...].astype(F32).reshape(tokens, width)
    dh = dh_ref[0].astype(F32).reshape(tokens, width)
    s = jax.nn.sigmoid(g)
    d_up = (dh * (g * s)).astype(BF16)
    d_gate = (dh * u * s * (1.0 + g * (1.0 - s))).astype(BF16)
    gwg_ref[...] = jnp.dot(xt[...], d_gate, preferred_element_type=F32).astype(BF16)
    gwu_ref[...] = jnp.dot(xt[...], d_up, preferred_element_type=F32).astype(BF16)
    dims = (((1,), (1,)), ((), ()))
    acc[...] += lax.dot_general(d_gate, wg_ref[...], dims, preferred_element_type=F32) + lax.dot_general(
        d_up, wu_ref[...], dims, preferred_element_type=F32
    )

    @pl.when(step == pl.num_programs(0) - 1)
    def _():
        gin_ref[...] = acc[...].astype(BF16)


def down_kernel(og_ref, gate_ref, up_ref, after_ref, gwd_ref):
    tokens, dl = og_ref.shape
    width = gate_ref.shape[2]
    g = gate_ref[...].astype(F32).reshape(tokens, width)
    u = up_ref[...].astype(F32).reshape(tokens, width)
    hidden = (g * jax.nn.sigmoid(g) * u).astype(BF16)
    gwd_ref[...] = lax.dot_general(
        hidden, og_ref[...], (((0,), (0,)), ((), ())), preferred_element_type=F32
    ).astype(BF16)


def per_device(n, G, inputs, gate_pre, up_pre, out_grad, w_gate, w_up, w_down):
    dh, gates, ups, xs, ogs = exchange(n, G, inputs, out_grad, gate_pre, up_pre, w_down)
    K, _, rows, cw = dh.shape
    dl, ffl = w_gate.shape
    tokens = n * rows
    x = xs.reshape(tokens, dl)
    og = ogs.reshape(tokens, dl)
    width = 1024 if cw % 1024 == 0 else cw
    per = cw // width
    steps = ffl // width
    whole = pl.BlockSpec((tokens, dl), lambda k: (0, 0))
    act = pl.BlockSpec((n, rows, width), lambda k: (0, 0, k))
    wide = pl.BlockSpec((dl, width), lambda k: (0, k))
    gin, gwg, gwu = pl.pallas_call(
        gate_up_kernel,
        grid=(steps,),
        out_shape=(
            jax.ShapeDtypeStruct((tokens, dl), BF16),
            jax.ShapeDtypeStruct((dl, ffl), BF16),
            jax.ShapeDtypeStruct((dl, ffl), BF16),
        ),
        in_specs=[whole, pl.BlockSpec((1, n, rows, width), lambda k: (k // per, 0, 0, k % per)), act, act, wide, wide],
        out_specs=(whole, wide, wide),
        scratch_shapes=[pltpu.VMEM((dl, tokens), BF16), pltpu.VMEM((tokens, dl), F32)],
        compiler_params=pltpu.CompilerParams(vmem_limit_bytes=48 * 2**20),
        cost_estimate=pl.CostEstimate(flops=8 * tokens * dl * ffl, bytes_accessed=8 * dl * ffl, transcendentals=0),
    )(x, dh, gates, ups, w_gate, w_up)
    grad_input = lax.psum_scatter(gin, "gy", scatter_dimension=0, tiled=True)
    gwd = pl.pallas_call(
        down_kernel,
        grid=(steps,),
        out_shape=jax.ShapeDtypeStruct((ffl, dl), BF16),
        in_specs=[whole, act, act, pl.BlockSpec(memory_space=pl.ANY)],
        out_specs=pl.BlockSpec((width, dl), lambda k: (k, 0)),
        compiler_params=pltpu.CompilerParams(vmem_limit_bytes=48 * 2**20),
        cost_estimate=pl.CostEstimate(flops=2 * tokens * dl * ffl, bytes_accessed=2 * dl * ffl, transcendentals=0),
    )(og, gates, ups, gin)
    return grad_input, gwg, gwu, gwd


def solution(mesh):
    placed = (
        P("gy", "gx"),
        P("gx", "gy"),
        P("gx", "gy"),
        P("gy", "gx"),
        P("gx", "gy"),
        P("gx", "gy"),
        P("gy", "gx"),
    )
    return jax.shard_map(
        functools.partial(per_device, mesh.shape["gx"], mesh.shape["gy"]),
        mesh=mesh,
        in_specs=placed,
        out_specs=(P("gy", "gx"), P("gx", "gy"), P("gx", "gy"), P("gy", "gx")),
        check_vma=False,
    )
```

```python
import functools

import jax
import jax.numpy as jnp
from jax import lax
from jax.experimental import pallas as pl
from jax.experimental.pallas import tpu as pltpu
from jax.sharding import PartitionSpec as P

MESH = pl.DeviceIdType.MESH
F32 = jnp.float32
BF16 = jnp.bfloat16
CHUNKS = 7
OUTER = 4


def exchange_kernel(
    sizes,
    x_ref, og_ref, gate_ref, up_ref, wd_ref, wg_ref, wu_ref,
    gin_ref, dg_ref, du_ref, ht_ref, xs_ref, ogs_ref,
    dh_ref, gates_ref, ups_ref, factor_gate, factor_up, g_buf, u_buf, h_out, g_out, u_out, acc,
    gu_sem, h_sem, out_sem,
    w_buf, og_buf, part, core_in, sum_core, inner_in, sum_inner, outer_in, own,
    w_sem, local_sem, gy_send, gy_recv,
    rc_send, rc_recv, ri_send, ri_recv, ro_send, ro_recv,
    go_send, go_recv, gi_send, gi_recv, gc_send, gc_recv,
    ho_send, ho_recv, hi_send, hi_recv, hc_send, hc_recv,
    own_sem,
):
    A, B, G, K = sizes
    me = lax.axis_index("gx")
    gy = lax.axis_index("gy")
    core = lax.rem(me, 2)
    b = lax.rem(me // 2, B)
    a = me // (2 * B)
    cw = w_buf.shape[1]
    t = og_ref.shape[0]

    def index(ai, bi, ci):
        return (ai * B + bi) * 2 + ci

    def outer_peer(d):
        return lax.rem(a + d, A)

    def outer_source(d):
        return lax.rem(a + A - d, A)

    def inner_peer(d):
        return lax.rem(b + d, B)

    def inner_source(d):
        return lax.rem(b + B - d, B)

    def remote(src, dst, send, recv, gx_to, gy_to=None):
        return pltpu.make_async_remote_copy(
            src_ref=src, dst_ref=dst, send_sem=send, recv_sem=recv,
            device_id=(gx_to, gy if gy_to is None else gy_to), device_id_type=MESH,
        )

    sibling = index(a, b, 1 - core)

    barrier = pltpu.get_barrier_semaphore()
    pl.semaphore_signal(barrier, inc=1, device_id=(sibling, gy), device_id_type=MESH)
    for d in range(1, A):
        pl.semaphore_signal(barrier, inc=1, device_id=(index(outer_peer(d), b, core), gy), device_id_type=MESH)
    for d in range(1, B):
        pl.semaphore_signal(barrier, inc=1, device_id=(index(a, inner_peer(d), core), gy), device_id_type=MESH)
    for d in range(1, G):
        pl.semaphore_signal(barrier, inc=1, device_id=(me, lax.rem(gy + d, G)), device_id_type=MESH)
    pl.semaphore_wait(barrier, 1 + (A - 1) + (B - 1) + (G - 1))

    def w_copy(k, slot):
        return pltpu.make_async_copy(wd_ref.at[pl.ds(pl.multiple_of(k * cw, cw), cw)], w_buf.at[slot], w_sem.at[slot])

    w_copy(0, 0).start()
    w_copy(1, 1).start()

    def gy_copy(i, d):
        to = lax.rem(gy + d, G)
        src, dst = ((og_ref, og_buf), (x_ref, xs_ref))[i]
        return remote(src, dst.at[gy], gy_send.at[i, d - 1], gy_recv.at[i, d - 1], me, to)

    locals_ = [
        pltpu.make_async_copy(og_ref, og_buf.at[gy], local_sem.at[0]),
        pltpu.make_async_copy(x_ref, xs_ref.at[gy], local_sem.at[1]),
        pltpu.make_async_copy(gate_ref, gates_ref.at[me], local_sem.at[2]),
        pltpu.make_async_copy(up_ref, ups_ref.at[me], local_sem.at[3]),
    ]
    locals_[0].start()
    for d in range(1, G):
        gy_copy(0, d).start()

    def gather_ops(full, outer_s, outer_r, inner_s, inner_r, core_s, core_r):
        def to_outer(src, d):
            return remote(src, full(me), outer_s(d - 1), outer_r(d - 1), index(outer_peer(d), b, core))

        def to_inner(src, ai, d):
            s = index(ai, b, core)
            return remote(src, full(s), inner_s(d - 1, ai), inner_r(d - 1, ai), index(a, inner_peer(d), core))

        def to_core(src, ai, bi):
            s = index(ai, bi, core)
            return remote(src, full(s), core_s(ai * B + bi), core_r(ai * B + bi), sibling)

        return to_outer, to_inner, to_core

    def send_own(ops, src):
        to_outer, to_inner, to_core = ops
        for d in range(1, A):
            to_outer(src, d).start()
        for d in range(1, B):
            to_inner(src, a, d).start()
        to_core(src, a, b).start()

    def pass_outer(ops, full):
        to_outer, to_inner, to_core = ops
        for d in range(1, A):
            to_outer(full(me), d).wait_recv()
            ai = outer_source(d)
            src = full(index(ai, b, core))
            for e in range(1, B):
                to_inner(src, ai, e).start()
            to_core(src, ai, b).start()

    def pass_inner(ops, full):
        to_outer, to_inner, to_core = ops
        for e in range(1, B):
            bi = inner_source(e)
            for d in range(A):
                ai = outer_source(d)
                to_inner(full(me), ai, e).wait_recv()
                to_core(full(index(ai, bi, core)), ai, bi).start()

    def finish_sends(ops, full):
        to_outer, to_inner, to_core = ops
        for d in range(1, A):
            to_outer(full(me), d).wait_send()
        for e in range(1, B):
            for ai in range(A):
                to_inner(full(me), ai, e).wait_send()
        for ai in range(A):
            for bi in range(B):
                to_core(full(me), ai, bi).wait_send()

    def finish_core(ops, full):
        to_outer, to_inner, to_core = ops
        for ai in range(A):
            for bi in range(B):
                to_core(full(me), ai, bi).wait_recv()

    saved = []
    for g, out in enumerate((gates_ref, ups_ref)):
        full = functools.partial(lambda out, s: out.at[s], out)
        ops = gather_ops(
            full,
            functools.partial(lambda g, i: go_send.at[g, i], g),
            functools.partial(lambda g, i: go_recv.at[g, i], g),
            functools.partial(lambda g, i, j: gi_send.at[g, i, j], g),
            functools.partial(lambda g, i, j: gi_recv.at[g, i, j], g),
            functools.partial(lambda g, i: gc_send.at[g, i], g),
            functools.partial(lambda g, i: gc_recv.at[g, i], g),
        )
        saved.append((ops, full))

    send_own(saved[0][0], gate_ref)
    send_own(saved[1][0], up_ref)
    for d in range(1, G):
        gy_copy(1, d).start()
    for copy in locals_[1:]:
        copy.start()
    locals_[0].wait()
    for d in range(1, G):
        gy_copy(0, d).wait_recv()
    og_out = pltpu.make_async_copy(og_buf, ogs_ref, local_sem.at[4])
    og_out.start()

    def core_copy(k):
        return remote(part.at[k, :, :, 1 - core], core_in.at[k], rc_send.at[k], rc_recv.at[k], sibling)

    def inner_copy(k, e):
        return remote(
            sum_core.at[k, inner_peer(e)], inner_in.at[k, e - 1],
            ri_send.at[k, e - 1], ri_recv.at[k, e - 1], index(a, inner_peer(e), core),
        )

    def outer_copy(k, d):
        return remote(
            sum_inner.at[k, outer_peer(d)], outer_in.at[k, d - 1],
            ro_send.at[k, d - 1], ro_recv.at[k, d - 1], index(outer_peer(d), b, core),
        )

    def multiply(k, _):
        slot = lax.rem(k, 2)
        w_copy(k, slot).wait()
        og = og_buf[...].reshape(G * t, og_buf.shape[2])
        prod = lax.dot_general(og, w_buf[slot], (((1,), (1,)), ((), ())), preferred_element_type=F32)
        part[k] = prod.reshape(part.shape[1:]).astype(BF16)
        core_copy(k).start()

        @pl.when(k + 2 < K)
        def _():
            w_copy(k + 2, slot).start()
        return 0

    lax.fori_loop(0, K, multiply, 0)

    def add_core(k, _):
        core_copy(k).wait_recv()
        for bi in range(B):
            sum_core[k, bi] = (part[k, :, bi, core].astype(F32) + core_in[k, :, bi].astype(F32)).astype(BF16)
        for e in range(1, B):
            inner_copy(k, e).start()
        return 0

    lax.fori_loop(0, K, add_core, 0)
    for ops, full in saved:
        pass_outer(ops, full)

    def add_inner(k, _):
        total = sum_core[k, b].astype(F32)
        for e in range(1, B):
            inner_copy(k, e).wait_recv()
            total += inner_in[k, e - 1].astype(F32)
        sum_inner[k] = total.astype(BF16)
        for d in range(1, A):
            outer_copy(k, d).start()
        return 0

    lax.fori_loop(0, K, add_inner, 0)
    for ops, full in saved:
        pass_inner(ops, full)

    def hidden_ops(k):
        full = lambda s: dh_ref.at[k, s]
        return gather_ops(
            full,
            lambda i: ho_send.at[k, i], lambda i: ho_recv.at[k, i],
            lambda i, j: hi_send.at[k, i, j], lambda i, j: hi_recv.at[k, i, j],
            lambda i: hc_send.at[k, i], lambda i: hc_recv.at[k, i],
        ), full

    def own_copy(k):
        return pltpu.make_async_copy(own.at[k], dh_ref.at[k, me], own_sem.at[k])

    def add_outer(k, _):
        total = sum_inner[k, a].astype(F32)
        for d in range(1, A):
            outer_copy(k, d).wait_recv()
            total += outer_in[k, d - 1].astype(F32)
        own[k] = total.astype(BF16)
        send_own(hidden_ops(k)[0], own.at[k])
        own_copy(k).start()
        return 0

    lax.fori_loop(0, K, add_outer, 0)

    tokens = G * t
    dl = og_ref.shape[1]

    def columns(k):
        return pl.ds(pl.multiple_of(k * cw, cw), cw)

    def weight_copies(k, slot):
        return (
            pltpu.make_async_copy(wg_ref.at[:, columns(k)], g_buf.at[slot], gu_sem.at[0, slot]),
            pltpu.make_async_copy(wu_ref.at[:, columns(k)], u_buf.at[slot], gu_sem.at[1, slot]),
        )

    def start_weights(k, slot):
        for copy in weight_copies(k, slot):
            copy.start()

    def h_copy(k, slot):
        return pltpu.make_async_copy(h_out.at[slot], ht_ref.at[columns(k)], h_sem.at[slot])

    start_weights(0, 0)
    start_weights(1, 1)
    for copy in locals_[2:]:
        copy.wait()
    for ops, full in saved:
        finish_core(ops, full)
    acc[...] = jnp.zeros_like(acc)

    def prepare(k):
        slot = lax.rem(k, 2)
        g = gates_ref[:, :, columns(k)].astype(F32).reshape(tokens, cw)
        u = ups_ref[:, :, columns(k)].astype(F32).reshape(tokens, cw)
        s = jax.nn.sigmoid(g)
        silu = g * s
        factor_up[k] = silu
        factor_gate[k] = u * s * (1.0 + g * (1.0 - s))

        @pl.when(k >= 2)
        def _():
            h_copy(k - 2, slot).wait()
        h_out[slot] = (silu * u).T.astype(BF16)
        h_copy(k, slot).start()

    def forward_outer(k, _):
        pass_outer(*hidden_ops(k))
        prepare(k)
        return 0

    lax.fori_loop(0, K, forward_outer, 0)

    def out_copies(k, slot):
        return (
            pltpu.make_async_copy(g_out.at[slot], dg_ref.at[:, columns(k)], out_sem.at[0, slot]),
            pltpu.make_async_copy(u_out.at[slot], du_ref.at[:, columns(k)], out_sem.at[1, slot]),
        )

    def process(k):
        slot = lax.rem(k, 2)
        finish_core(*hidden_ops(k))
        own_copy(k).wait()
        dh = dh_ref[k].astype(F32).reshape(tokens, cw)

        @pl.when(k >= 2)
        def _():
            for copy in out_copies(k - 2, slot):
                copy.wait()
        g_out[slot] = (dh * factor_gate[k]).astype(BF16)
        u_out[slot] = (dh * factor_up[k]).astype(BF16)
        for copy in out_copies(k, slot):
            copy.start()
        for copy in weight_copies(k, slot):
            copy.wait()
        dims = (((1,), (1,)), ((), ()))
        acc[...] += lax.dot_general(g_out[slot], g_buf[slot], dims, preferred_element_type=F32)
        acc[...] += lax.dot_general(u_out[slot], u_buf[slot], dims, preferred_element_type=F32)

        @pl.when(k + 2 < K)
        def _():
            start_weights(k + 2, slot)

    def forward_inner(k, _):
        @pl.when(k < K)
        def _():
            pass_inner(*hidden_ops(k))

        @pl.when(k >= 1)
        def _():
            process(k - 1)
        return 0

    lax.fori_loop(0, K + 1, forward_inner, 0)
    gin_ref[...] = acc[...].astype(BF16)

    def close(k, _):
        finish_sends(*hidden_ops(k))
        core_copy(k).wait_send()
        for e in range(1, B):
            inner_copy(k, e).wait_send()
        for d in range(1, A):
            outer_copy(k, d).wait_send()
        return 0

    lax.fori_loop(0, K, close, 0)
    for k in (K - 2, K - 1):
        h_copy(k, k % 2).wait()
        for copy in out_copies(k, k % 2):
            copy.wait()
    for ops, full in saved:
        finish_sends(ops, full)
    locals_[1].wait()
    og_out.wait()
    for d in range(1, G):
        gy_copy(0, d).wait_send()
        gy_copy(1, d).wait()


def exchange(n, G, x, og, gate, up, wd, wg, wu):
    A = OUTER if n % (2 * OUTER) == 0 else 1
    B = n // (2 * A)
    K = CHUNKS
    t, dl = og.shape
    rows, ffl = gate.shape
    cw = ffl // K
    any_spec = pl.BlockSpec(memory_space=pl.ANY)
    dma = pltpu.SemaphoreType.DMA
    return pl.pallas_call(
        functools.partial(exchange_kernel, (A, B, G, K)),
        out_shape=(
            jax.ShapeDtypeStruct((G * t, dl), BF16),
            jax.ShapeDtypeStruct((G * t, ffl), BF16),
            jax.ShapeDtypeStruct((G * t, ffl), BF16),
            jax.ShapeDtypeStruct((ffl, G * t), BF16),
            jax.ShapeDtypeStruct((G, t, dl), BF16),
            jax.ShapeDtypeStruct((G, t, dl), BF16),
        ),
        in_specs=[any_spec] * 7,
        out_specs=(pl.BlockSpec(memory_space=pltpu.VMEM),) + (any_spec,) * 5,
        scratch_shapes=[
            pltpu.VMEM((K, n, rows, cw), BF16),
            pltpu.VMEM((n, rows, ffl), BF16),
            pltpu.VMEM((n, rows, ffl), BF16),
            pltpu.VMEM((K, G * t, cw), F32),
            pltpu.VMEM((K, G * t, cw), F32),
            pltpu.VMEM((2, dl, cw), BF16),
            pltpu.VMEM((2, dl, cw), BF16),
            pltpu.VMEM((2, cw, G * t), BF16),
            pltpu.VMEM((2, G * t, cw), BF16),
            pltpu.VMEM((2, G * t, cw), BF16),
            pltpu.VMEM((G * t, dl), F32),
            dma((2, 2)), dma((2,)), dma((2, 2)),
            pltpu.VMEM((2, cw, dl), BF16),
            pltpu.VMEM((G, t, dl), BF16),
            pltpu.VMEM((K, A, B, 2, rows, cw), BF16),
            pltpu.VMEM((K, A, B, rows, cw), BF16),
            pltpu.VMEM((K, B, A, rows, cw), BF16),
            pltpu.VMEM((K, max(B - 1, 1), A, rows, cw), BF16),
            pltpu.VMEM((K, A, rows, cw), BF16),
            pltpu.VMEM((K, max(A - 1, 1), rows, cw), BF16),
            pltpu.VMEM((K, rows, cw), BF16),
            dma((2,)), dma((5,)), dma((2, max(G - 1, 1))), dma((2, max(G - 1, 1))),
            dma((K,)), dma((K,)), dma((K, max(B - 1, 1))), dma((K, max(B - 1, 1))),
            dma((K, max(A - 1, 1))), dma((K, max(A - 1, 1))),
            dma((2, max(A - 1, 1))), dma((2, max(A - 1, 1))),
            dma((2, max(B - 1, 1), A)), dma((2, max(B - 1, 1), A)),
            dma((2, A * B)), dma((2, A * B)),
            dma((K, max(A - 1, 1))), dma((K, max(A - 1, 1))),
            dma((K, max(B - 1, 1), A)), dma((K, max(B - 1, 1), A)),
            dma((K, A * B)), dma((K, A * B)),
            dma((K,)),
        ],
        compiler_params=pltpu.CompilerParams(
            collective_id=0, has_side_effects=True, vmem_limit_bytes=62 * 2**20
        ),
    )(x, og, gate, up, wd, wg, wu)


def weights_kernel(x_ref, og_ref, dg_ref, du_ref, ht_ref, gwg_ref, gwu_ref, gwd_ref, xt):
    @pl.when(pl.program_id(0) == 0)
    def _():
        xt[...] = x_ref[...].astype(F32).T.astype(BF16)

    gwg_ref[...] = jnp.dot(xt[...], dg_ref[...], preferred_element_type=F32).astype(BF16)
    gwu_ref[...] = jnp.dot(xt[...], du_ref[...], preferred_element_type=F32).astype(BF16)
    gwd_ref[...] = jnp.dot(ht_ref[...], og_ref[...], preferred_element_type=F32).astype(BF16)


def per_device(n, G, inputs, gate_pre, up_pre, out_grad, w_gate, w_up, w_down):
    gin, dg, du, ht, xs, ogs = exchange(n, G, inputs, out_grad, gate_pre, up_pre, w_down, w_gate, w_up)
    dl, ffl = w_gate.shape
    tokens = dg.shape[0]
    grad_input = lax.psum_scatter(gin, "gy", scatter_dimension=0, tiled=True)
    width = 1024 if ffl % 1024 == 0 else 512
    whole = pl.BlockSpec((tokens, dl), lambda k: (0, 0))
    act = pl.BlockSpec((tokens, width), lambda k: (0, k))
    wide = pl.BlockSpec((dl, width), lambda k: (0, k))
    gwg, gwu, gwd = pl.pallas_call(
        weights_kernel,
        grid=(ffl // width,),
        out_shape=(
            jax.ShapeDtypeStruct((dl, ffl), BF16),
            jax.ShapeDtypeStruct((dl, ffl), BF16),
            jax.ShapeDtypeStruct((ffl, dl), BF16),
        ),
        in_specs=[
            whole, whole, act, act,
            pl.BlockSpec((width, tokens), lambda k: (k, 0)),
        ],
        out_specs=(wide, wide, pl.BlockSpec((width, dl), lambda k: (k, 0))),
        scratch_shapes=[pltpu.VMEM((dl, tokens), BF16)],
        compiler_params=pltpu.CompilerParams(vmem_limit_bytes=62 * 2**20),
        cost_estimate=pl.CostEstimate(flops=6 * tokens * dl * ffl, bytes_accessed=8 * dl * ffl, transcendentals=0),
    )(xs.reshape(tokens, dl), ogs.reshape(tokens, dl), dg, du, ht)
    return grad_input, gwg, gwu, gwd


def solution(mesh):
    placed = (
        P("gy", "gx"),
        P("gx", "gy"),
        P("gx", "gy"),
        P("gy", "gx"),
        P("gx", "gy"),
        P("gx", "gy"),
        P("gy", "gx"),
    )
    return jax.shard_map(
        functools.partial(per_device, mesh.shape["gx"], mesh.shape["gy"]),
        mesh=mesh,
        in_specs=placed,
        out_specs=(P("gy", "gx"), P("gx", "gy"), P("gx", "gy"), P("gy", "gx")),
        check_vma=False,
    )
```
